32 devices in a mesh: groups: 2 (over x), space: 16 (over z, y, core).
Axes of the slice: x: 2, y: 2, z: 4, core: 2. Of those that a mesh axis runs over, the one named last changes fastest.
Arguments:
- eigvecs: bfloat16 [4, 2, 3, 16, 128, 256], P('groups', None, None, 'space'), parts along dimension 0, may hold values from -12 to 12
- links: bfloat16 [4, 3, 2, 3, 3, 16, 128], P('groups', None, None, None, None, 'space'), parts along dimension 0, may hold values from -4 to 4
- directions: int32 [4], P('groups'), parts along dimension 0, may hold values from 0 to 2
- pairs: int32 [128, 2], P(('groups', 'space')), parts along dimension 0, may hold values from 0 to 1
- perambulators: bfloat16 [128, 2, 256, 256], P(('groups', 'space')), parts along dimension 0, may hold values from -0.25 to 0.25
Outputs:
- elementals: float32 [4, 2, 2, 256, 256], P('groups', None, None, 'space'), parts along dimension 0
- pair_matrices: bfloat16 [128, 2, 256, 256], P(('groups', 'space')), parts along dimension 0
The draws below stay inside these ranges and needn't reach their ends.
There are 2 independent parts, one for each index of `groups`. The reference program is written for one: setup_inputs(seed, part) draws one part's arguments, and reference() takes and returns one part's arrays. A program takes and returns all parts, laid end to end along the dimension named above; each array names one. Nothing has to cross between parts.
Inputs may be any that keep to these rules, and one draw needn't show every extreme that they name: `directions`: 0 is x, 1 is y, 2 is z. pairs[p, 0] is the source time slice and pairs[p, 1] the sink time slice of pair p.
All inputs are finite; a program needn't handle non-finite values.
Results may differ from the reference program's by a relative error of at most 0.011.
Values may be sent and summed in bfloat16 or wider, within the bound.
A program may use at most 64 MiB of HBM per device.

```python
import jax
import jax.numpy as jnp
from jax import lax

NVEC = 256
TSL = 2
LX = 16
LY = 8
NZ = 16
PAIRS = 64


def with_ends(values, key, low, largest):
    index_at = [jax.random.randint(jax.random.fold_in(key, axis), (), 0, length) for axis, length in enumerate(values.shape)]
    widest = values.shape.index(max(values.shape))
    beside = index_at[:widest] + [(index_at[widest] + 1) % values.shape[widest]] + index_at[widest + 1:]
    return values.at[tuple(index_at)].set(low).at[tuple(beside)].set(largest)


def level_of(key, shape, pieces, smallest, largest):
    factor_of = 1.0
    for position, parts in pieces:
        heights = jax.random.uniform(jax.random.fold_in(jax.random.fold_in(key, 6), position), (parts,), jnp.float32, smallest / len(pieces), largest / len(pieces))
        factor_of = factor_of * jnp.repeat(jnp.exp(heights), shape[position] // parts).reshape((-1,) + (1,) * (len(shape) - 1 - position))
    return factor_of


def centred(own_key, shape, width, reach, shards=(), kind=jnp.bfloat16):
    array = jax.random.normal(own_key, shape, jnp.float32) * width
    if len(shards) > 0:
        array = level_of(own_key, shape, shards, -0.22, 0.18) * array
    return jnp.clip(array, min=-reach, max=reach).astype(kind)


def setup_inputs(seed: int = 0, part: int = 0) -> dict:
    arg_keys = jax.random.split(jax.random.key(seed), 6)
    own_keys = jax.random.split(jax.random.fold_in(arg_keys[5], part), 6)
    eigvecs = centred(own_keys[0], (TSL, 2, 3, NZ, LX * LY, NVEC), 2.0, 12.0, ((3, 16),))
    links = centred(own_keys[1], (TSL, 3, 2, 3, 3, NZ, LX * LY), 0.577, 4.0, ((5, 16),))
    directions = jax.random.randint(own_keys[2], (2,), 0, 3).astype(jnp.int32)
    pairs = with_ends(jax.random.randint(own_keys[3], (PAIRS, 2), 0, TSL), jax.random.fold_in(own_keys[3], 1), 0, TSL - 1).astype(jnp.int32)
    perambulators = centred(own_keys[4], (PAIRS, 2, NVEC, NVEC), (2 * NVEC) ** -0.5, 0.25, ((0, 16),))
    return {"eigvecs": eigvecs, "links": links, "directions": directions, "pairs": pairs, "perambulators": perambulators}


smear_weight = 0.12
vector_axes = (3, 4, 2)
link_axes = (4, 5, 3)


def forward_hop(gauge_link, vectors):
    real_parts = []
    imag_parts = []
    for out_color in range(3):
        real_sum = jnp.zeros(vectors.shape[2:], jnp.float32)
        imag_sum = jnp.zeros(vectors.shape[2:], jnp.float32)
        for in_color in range(3):
            link_real = gauge_link[0, out_color, in_color][..., None]
            link_imag = gauge_link[1, out_color, in_color][..., None]
            field_real = vectors[0, in_color].astype(jnp.float32)
            field_imag = vectors[1, in_color].astype(jnp.float32)
            real_sum = real_sum + link_real * field_real - link_imag * field_imag
            imag_sum = imag_sum + link_real * field_imag + link_imag * field_real
        real_parts.append(real_sum)
        imag_parts.append(imag_sum)
    return jnp.stack([jnp.stack(real_parts), jnp.stack(imag_parts)])


def backward_hop(gauge_link, vectors):
    real_parts = []
    imag_parts = []
    for out_color in range(3):
        real_sum = jnp.zeros(vectors.shape[2:], jnp.float32)
        imag_sum = jnp.zeros(vectors.shape[2:], jnp.float32)
        for in_color in range(3):
            link_real = gauge_link[0, in_color, out_color][..., None]
            link_imag = gauge_link[1, in_color, out_color][..., None]
            field_real = vectors[0, in_color].astype(jnp.float32)
            field_imag = vectors[1, in_color].astype(jnp.float32)
            real_sum = real_sum + link_real * field_real + link_imag * field_imag
            imag_sum = imag_sum + link_real * field_imag - link_imag * field_real
        real_parts.append(real_sum)
        imag_parts.append(imag_sum)
    return jnp.stack([jnp.stack(real_parts), jnp.stack(imag_parts)])


def inner_product(left_side, right_side):
    return lax.dot_general(left_side, right_side, (((0,), (0,)), ((), ())), preferred_element_type=jnp.float32)


def plain_dot(left_side, right_side):
    return jnp.dot(left_side, right_side, preferred_element_type=jnp.float32)


def complex_product(left_side, right_side):
    real_part = plain_dot(left_side[0], right_side[0]) - plain_dot(left_side[1], right_side[1])
    imag_part = plain_dot(left_side[0], right_side[1]) + plain_dot(left_side[1], right_side[0])
    return jnp.stack([real_part, imag_part])


def adjoint_product(left_side, right_side):
    real_part = plain_dot(left_side[0], right_side[0].T) + plain_dot(left_side[1], right_side[1].T)
    imag_part = plain_dot(left_side[1], right_side[0].T) - plain_dot(left_side[0], right_side[1].T)
    return jnp.stack([real_part, imag_part])


def slice_terms(eigen_slice, link_slice, directions):
    vectors = eigen_slice.reshape(2, 3, NZ, LX, LY, NVEC)
    gauge_field = link_slice.astype(jnp.float32).reshape(3, 2, 3, 3, NZ, LX, LY)
    ahead_links = [gauge_field[direction] for direction in range(3)]
    behind_links = [jnp.roll(gauge_field[direction], 1, link_axes[direction]) for direction in range(3)]

    def laplace_step(current):
        laplace_sum = -6.0 * current.astype(jnp.float32)
        for direction in range(3):
            ahead_field = jnp.roll(current, -1, vector_axes[direction])
            behind = jnp.roll(current, 1, vector_axes[direction])
            laplace_sum = laplace_sum + forward_hop(ahead_links[direction], ahead_field) + backward_hop(behind_links[direction], behind)
        return (current.astype(jnp.float32) + smear_weight * laplace_sum).astype(jnp.bfloat16)

    def displace_along(direction):
        def displaced(smeared):
            ahead_field = jnp.roll(smeared, -1, vector_axes[direction])
            behind = jnp.roll(smeared, 1, vector_axes[direction])
            return (forward_hop(ahead_links[direction], ahead_field) - backward_hop(behind_links[direction], behind)).astype(jnp.bfloat16)
        return displaced

    branches = [displace_along(direction) for direction in range(3)]
    smeared = laplace_step(laplace_step(vectors))
    site_rows = 3 * NZ * LX * LY
    smeared_rows = smeared.reshape(2, site_rows, NVEC)
    blocks = []
    for copy_index in range(2):
        shifted_rows = lax.switch(directions[copy_index], branches, smeared).reshape(2, site_rows, NVEC)
        real_part = inner_product(smeared_rows[0], shifted_rows[0]) + inner_product(smeared_rows[1], shifted_rows[1])
        imag_part = inner_product(smeared_rows[0], shifted_rows[1]) - inner_product(smeared_rows[1], shifted_rows[0])
        blocks.append(jnp.stack([real_part, imag_part]))
    return jnp.stack(blocks)


def reference(eigvecs, links, directions, pairs, perambulators):
    site_scale = (6.0 * NZ * LX * LY) ** -0.5
    pair_scale = (2.0 * NVEC) ** -0.5

    def per_slice(operands):
        return slice_terms(operands[0], operands[1], directions) * site_scale

    elementals = lax.map(per_slice, (eigvecs, links))
    panels = elementals.astype(jnp.bfloat16)

    def per_pair(operands):
        pair_row = operands[0]
        propagator = operands[1]
        left_side = panels[pair_row[1], 0]
        right_side = panels[pair_row[0], 1]
        first_product = complex_product(left_side, propagator).astype(jnp.bfloat16)
        second_product = (complex_product(first_product, right_side) * pair_scale).astype(jnp.bfloat16)
        return adjoint_product(second_product, propagator).astype(jnp.bfloat16)

    pair_matrices = lax.map(per_pair, (pairs, perambulators))
    return elementals, pair_matrices
```

```python
import functools

import jax
import jax.numpy as jnp
from jax import lax
from jax.experimental import pallas as pl
from jax.experimental.pallas import tpu as pltpu
from jax.sharding import PartitionSpec as P

LX = 16
LY = 8
SITES = LX * LY
ROWS = 6 * SITES

smear_weight = 0.12
MESH = pl.DeviceIdType.MESH
F32 = jnp.float32
BF16 = jnp.bfloat16


def bit_reversed(value, bits):
    result = 0
    for bit in range(bits):
        result = result * 2 + (value >> bit) % 2
    return result


def put_complex(ref, lead, out_color, in_color, real_block, imag_block):
    top = slice(out_color * SITES, (out_color + 1) * SITES)
    low = slice((3 + out_color) * SITES, (4 + out_color) * SITES)
    left = slice(in_color * SITES, (in_color + 1) * SITES)
    right = slice((3 + in_color) * SITES, (4 + in_color) * SITES)
    real_block = real_block.astype(BF16)
    ref[(*lead, top, left)] = real_block
    ref[(*lead, low, right)] = real_block
    ref[(*lead, top, right)] = (-imag_block).astype(BF16)
    ref[(*lead, low, left)] = imag_block.astype(BF16)


def field_kernel(
    count,
    scale,
    directions_ref,
    eig_ref,
    links_ref,
    z_ref,
    owned_ref,
    panels_ref,
    z_below,
    columns,
    plane_ops,
    up_ops,
    down_ops,
    hop_ops,
    halo,
    first_field,
    final_field,
    accum,
    shifted,
    partial_sums,
    send_buf,
    recv_buf,
    gathered,
    link_send,
    link_recv,
    halo_send,
    halo_recv,
    sum_send,
    sum_recv,
    gather_send,
    gather_recv,
):
    slices = eig_ref.shape[0]
    nvec = eig_ref.shape[2]
    bits = count.bit_length() - 1
    owned = nvec // count
    me = lax.axis_index("space")
    above = (me + 1) % count
    below = (me + count - 1) % count
    my_bits = [(me // 2**bit) % 2 for bit in range(bits)]
    partners = [me + 2**bit * (1 - 2 * my_bits[bit]) for bit in range(bits)]

    barrier = pltpu.get_barrier_semaphore()
    greeted = [above, below] + partners
    for device in greeted:
        pl.semaphore_signal(barrier, inc=1, device_id={"space": device}, device_id_type=MESH)
    pl.semaphore_wait(barrier, len(greeted))

    def remote(source, target, send_sem, recv_sem, device):
        return pltpu.make_async_remote_copy(
            src_ref=source,
            dst_ref=target,
            send_sem=send_sem,
            recv_sem=recv_sem,
            device_id={"space": device},
            device_id_type=MESH,
        )

    pending = []

    def halo_copies(step, t):
        source = (eig_ref, first_field, final_field.at[0])[step].at[t]
        if step == 2:
            return [
                remote(
                    source,
                    final_field.at[1, t],
                    halo_send.at[step, 0, t],
                    halo_recv.at[step, 0, t],
                    below,
                )
            ]
        return [
            remote(
                source,
                halo.at[step, side, t],
                halo_send.at[step, side, t],
                halo_recv.at[step, side, t],
                (below, above)[side],
            )
            for side in range(2)
        ]

    link_copy = remote(z_ref, z_below, link_send, link_recv, above)
    link_copy.start()
    pending.append(link_copy)
    for t in range(slices):
        for copy in halo_copies(0, t):
            copy.start()
            pending.append(copy)

    row = lax.broadcasted_iota(jnp.int32, (SITES, SITES), 0)
    col = lax.broadcasted_iota(jnp.int32, (SITES, SITES), 1)

    def next_x(site):
        return (site + LY) % SITES

    def next_y(site):
        return (site // LY) * LY + (site + 1) % LY

    ahead_x = col == next_x(row)
    ahead_y = col == next_y(row)
    behind_x = row == next_x(col)
    behind_y = row == next_y(col)
    same = row == col

    def build_planes(t, carry):
        columns[...] = jnp.zeros(columns.shape, F32)
        columns[0:18, :] = links_ref[t, 0]
        columns[24:42, :] = links_ref[t, 1]
        turned = columns[...].T
        for c in range(3):
            for d in range(3):
                blocks = []
                for part, sign in ((0, 1.0), (1, -1.0)):
                    here = part * 9 + c * 3 + d
                    there = part * 9 + d * 3 + c
                    block = jnp.where(ahead_x, turned[:, here : here + 1], 0.0)
                    block = jnp.where(ahead_y, turned[:, 24 + here : 25 + here], block)
                    block = jnp.where(behind_x, sign * links_ref[t, 0, there : there + 1, :], block)
                    block = jnp.where(behind_y, sign * links_ref[t, 1, there : there + 1, :], block)
                    blocks.append(block)
                put_complex(plane_ops, (t,), c, d, *blocks)
                blocks = [
                    jnp.where(same, z_ref[t, p * 9 + c * 3 + d : p * 9 + c * 3 + d + 1, :], 0.0)
                    for p in range(2)
                ]
                put_complex(up_ops, (t,), c, d, *blocks)
        return carry

    def build_hops(index, carry):
        t = index // 2
        k = index % 2
        direction = directions_ref[k]
        target = jnp.where(direction == 0, next_x(col), jnp.where(direction == 1, next_y(col), col))
        reached = row == target
        own = links_ref.at[t]
        values = own[direction]
        for c in range(3):
            for d in range(3):
                there = d * 3 + c
                put_complex(
                    hop_ops,
                    (t, k),
                    c,
                    d,
                    jnp.where(reached, values[there : there + 1, :], 0.0),
                    jnp.where(reached, -values[9 + there : 10 + there, :], 0.0),
                )
        return carry

    def build_down(t, carry):
        for c in range(3):
            for d in range(3):
                there = d * 3 + c
                put_complex(
                    down_ops,
                    (t,),
                    c,
                    d,
                    jnp.where(same, z_below[t, there : there + 1, :], 0.0),
                    jnp.where(same, -z_below[t, 9 + there : 10 + there, :], 0.0),
                )
        return carry

    lax.fori_loop(0, slices, build_planes, 0)
    lax.fori_loop(0, 2 * slices, build_hops, 0)
    link_copy.wait_recv()
    lax.fori_loop(0, slices, build_down, 0)

    def dot(left_side, right_side):
        return jnp.dot(left_side, right_side, preferred_element_type=F32)

    for step in range(2):
        current = (eig_ref, first_field)[step]

        def plane_part(t, carry, current=current):
            accum[t] = dot(plane_ops[t], current[t])
            return carry

        lax.fori_loop(0, slices, plane_part, 0)
        for t in range(slices):
            for copy in halo_copies(step, t):
                copy.wait_recv()
            total = (
                accum[t]
                + dot(up_ops[t], halo[step, 0, t])
                + dot(down_ops[t], halo[step, 1, t])
            )
            center = current[t].astype(F32)
            smeared = (center + smear_weight * (total - 6.0 * center)).astype(BF16)
            if step == 0:
                first_field[t] = smeared
            else:
                final_field[0, t] = smeared
            for copy in halo_copies(step + 1, t):
                copy.start()
                pending.append(copy)

    def hop_part(index, carry):
        t = index // 2
        k = index % 2
        shifted[t, k] = dot(hop_ops[t, k], final_field[0, t]).astype(BF16)
        return carry

    lax.fori_loop(0, 2 * slices, hop_part, 0)

    def inner(left_side, right_side):
        return lax.dot_general(
            left_side, right_side, (((0,), (0,)), ((), ())), preferred_element_type=F32
        )

    for t in range(slices):
        for copy in halo_copies(2, t):
            copy.wait_recv()

    def sums(index, carry):
        t = index // 2
        k = index % 2
        which = jnp.where(directions_ref[k] == 2, 1, 0)
        field = final_field[which, t]
        hopped = shifted[t, k]
        half = ROWS // 2
        real_part = inner(hopped, field)
        imag_part = inner(hopped[:half], field[half:]) - inner(hopped[half:], field[:half])
        real_part = real_part - real_part.T
        imag_part = imag_part + imag_part.T
        for block in range(count):
            place = bit_reversed(block, bits)
            rows = slice(block * owned, (block + 1) * owned)
            partial_sums[place, 2 * index] = real_part[rows]
            partial_sums[place, 2 * index + 1] = imag_part[rows]
        return carry

    lax.fori_loop(0, 2 * slices, sums, 0)

    base = 0
    size = count
    for bit in range(bits):
        size //= 2
        kept = base + my_bits[bit] * size
        given = base + (1 - my_bits[bit]) * size
        offset = count - 2 * size
        window = pl.ds(offset, size)
        send_buf[window] = partial_sums[pl.ds(given, size)].astype(BF16)
        copy = remote(
            send_buf.at[window],
            recv_buf.at[window],
            sum_send.at[bit],
            sum_recv.at[bit],
            partners[bit],
        )
        copy.start()
        pending.append(copy)
        copy.wait_recv()
        partial_sums[pl.ds(kept, size)] += recv_buf[window].astype(F32)
        base = kept

    own_rows = partial_sums[base] * scale
    owned_ref[...] = own_rows
    gathered[base] = own_rows.astype(BF16)
    size = 1
    for bit in reversed(range(bits)):
        start = (base // size) * size
        window = gathered.at[pl.ds(start, size)]
        copy = remote(
            window, window, gather_send.at[bit], gather_recv.at[bit], partners[bit]
        )
        copy.start()
        pending.append(copy)
        copy.wait_recv()
        size *= 2
    for block in range(count):
        place = bit_reversed(block, bits)
        panels_ref[:, block * owned : (block + 1) * owned, :] = gathered[place]
    for copy in pending:
        copy.wait_send()


def pair_kernel(scale, pairs_ref, panels_ref, peram_ref, out_ref):
    p = pl.program_id(0)
    sink = pairs_ref[p, 1]
    source = pairs_ref[p, 0]

    def dot(left_side, right_side):
        return jnp.dot(left_side, right_side, preferred_element_type=F32)

    def dot_adjoint(left_side, right_side):
        return lax.dot_general(
            left_side, right_side, (((1,), (1,)), ((), ())), preferred_element_type=F32
        )

    left_real = panels_ref[sink * 4]
    left_imag = panels_ref[sink * 4 + 1]
    right_real = panels_ref[source * 4 + 2]
    right_imag = panels_ref[source * 4 + 3]
    peram_real = peram_ref[0, 0]
    peram_imag = peram_ref[0, 1]
    first_real = (dot(left_real, peram_real) - dot(left_imag, peram_imag)).astype(BF16)
    first_imag = (dot(left_real, peram_imag) + dot(left_imag, peram_real)).astype(BF16)
    second_real = dot(first_real, right_real) - dot(first_imag, right_imag)
    second_imag = dot(first_real, right_imag) + dot(first_imag, right_real)
    second_real = (second_real * scale).astype(BF16)
    second_imag = (second_imag * scale).astype(BF16)
    out_ref[0, 0] = (
        dot_adjoint(second_real, peram_real) + dot_adjoint(second_imag, peram_imag)
    ).astype(BF16)
    out_ref[0, 1] = (
        dot_adjoint(second_imag, peram_real) - dot_adjoint(second_real, peram_imag)
    ).astype(BF16)


def body(eigvecs, links, directions, pairs, perambulators):
    slices = eigvecs.shape[0]
    planes = eigvecs.shape[3]
    nvec = eigvecs.shape[5]
    count = lax.axis_size("space")
    bits = count.bit_length() - 1
    owned = nvec // count
    assert planes == 1 and 2**bits == count
    eig = eigvecs.reshape(slices, ROWS, nvec)
    link_rows = links.astype(F32).reshape(slices, 3, 18, SITES)
    site_scale = (6.0 * planes * count * LX * LY) ** (-0.5)
    vmem = pl.BlockSpec(memory_space=pltpu.VMEM)
    smem = pl.BlockSpec(memory_space=pltpu.SMEM)
    dma = pltpu.SemaphoreType.DMA
    field = (slices, ROWS, nvec)
    square = (ROWS, ROWS)
    owned_rows, panels = pl.pallas_call(
        functools.partial(field_kernel, count, site_scale),
        out_shape=(
            jax.ShapeDtypeStruct((4 * slices, owned, nvec), F32),
            jax.ShapeDtypeStruct((4 * slices, nvec, nvec), BF16),
        ),
        in_specs=[smem, vmem, vmem, vmem],
        out_specs=(vmem, vmem),
        scratch_shapes=[
            pltpu.VMEM((slices, 18, SITES), F32),
            pltpu.VMEM((SITES, SITES), F32),
            pltpu.VMEM((slices, *square), BF16),
            pltpu.VMEM((slices, *square), BF16),
            pltpu.VMEM((slices, *square), BF16),
            pltpu.VMEM((slices, 2, *square), BF16),
            pltpu.VMEM((2, 2, *field), BF16),
            pltpu.VMEM(field, BF16),
            pltpu.VMEM((2, *field), BF16),
            pltpu.VMEM(field, F32),
            pltpu.VMEM((slices, 2, ROWS, nvec), BF16),
            pltpu.VMEM((count, 4 * slices, owned, nvec), F32),
            pltpu.VMEM((count, 4 * slices, owned, nvec), BF16),
            pltpu.VMEM((count, 4 * slices, owned, nvec), BF16),
            pltpu.VMEM((count, 4 * slices, owned, nvec), BF16),
            dma,
            dma,
            dma((3, 2, slices)),
            dma((3, 2, slices)),
            dma((bits,)),
            dma((bits,)),
            dma((bits,)),
            dma((bits,)),
        ],
        compiler_params=pltpu.CompilerParams(
            collective_id=0, has_side_effects=True, vmem_limit_bytes=60000 * 1024
        ),
        name="fields",
    )(directions, eig, link_rows, link_rows[:, 2])

    pair_scale = (2.0 * nvec) ** (-0.5)
    local_pairs = perambulators.shape[0]
    pair_matrices = pl.pallas_call(
        functools.partial(pair_kernel, pair_scale),
        out_shape=jax.ShapeDtypeStruct(perambulators.shape, BF16),
        grid=(local_pairs,),
        in_specs=[
            smem,
            pl.BlockSpec((4 * slices, nvec, nvec), lambda p: (0, 0, 0)),
            pl.BlockSpec((1, 2, nvec, nvec), lambda p: (p, 0, 0, 0)),
        ],
        out_specs=pl.BlockSpec((1, 2, nvec, nvec), lambda p: (p, 0, 0, 0)),
        name="pairs",
    )(pairs, panels, perambulators)
    return owned_rows.reshape(slices, 2, 2, owned, nvec), pair_matrices


def solution(mesh):
    placed = (
        P("groups", None, None, "space", None, None),
        P("groups", None, None, None, None, "space", None),
        P("groups"),
        P(("groups", "space"), None),
        P(("groups", "space"), None, None, None),
    )
    return jax.shard_map(
        body,
        mesh=mesh,
        in_specs=placed,
        out_specs=(
            P("groups", None, None, "space", None),
            P(("groups", "space"), None, None, None),
        ),
        check_vma=False,
    )
```

```python
import functools

import jax
import jax.numpy as jnp
from jax import lax
from jax.experimental import pallas as pl
from jax.experimental.pallas import tpu as pltpu
from jax.sharding import PartitionSpec as P

LX = 16
LY = 8
SITES = LX * LY
ROWS = 6 * SITES

smear_weight = 0.12
MESH = pl.DeviceIdType.MESH
F32 = jnp.float32
BF16 = jnp.bfloat16


def place_of(value, order):
    result = 0
    for bit in order:
        result = result * 2 + (value >> bit) % 2
    return result


def put_complex(ref, lead, out_color, in_color, real_block, imag_block):
    top = slice(out_color * SITES, (out_color + 1) * SITES)
    low = slice((3 + out_color) * SITES, (4 + out_color) * SITES)
    left = slice(in_color * SITES, (in_color + 1) * SITES)
    right = slice((3 + in_color) * SITES, (4 + in_color) * SITES)
    real_block = real_block.astype(BF16)
    ref[(*lead, top, left)] = real_block
    ref[(*lead, low, right)] = real_block
    ref[(*lead, top, right)] = (-imag_block).astype(BF16)
    ref[(*lead, low, left)] = imag_block.astype(BF16)


def field_kernel(
    count,
    scale,
    directions_ref,
    eig_ref,
    links_ref,
    owned_ref,
    panels_ref,
    z_below,
    columns,
    plane_ops,
    up_ops,
    down_ops,
    hop_ops,
    halo,
    first_field,
    final_field,
    accum,
    shifted,
    partial_sums,
    send_buf,
    recv_buf,
    gathered,
    planes,
    plane_links,
    spread_send,
    spread_recv,
    spread_link_send,
    spread_link_recv,
    link_send,
    link_recv,
    halo_send,
    halo_recv,
    sum_send,
    sum_recv,
    gather_send,
    gather_recv,
):
    slices = eig_ref.shape[0]
    nvec = eig_ref.shape[2]
    bits = count.bit_length() - 1
    owned = nvec // count
    me = lax.axis_index("space")
    my_bits = [(me // 2**bit) % 2 for bit in range(bits)]
    partners = [me + 2**bit * (1 - 2 * my_bits[bit]) for bit in range(bits)]
    side, own_t = my_bits[0], my_bits[1]
    quad = (me // 4) * 4
    above = (me + 1 + 2 * side) % count
    below = (me + count - 3 + 2 * side) % count
    order = [0] + list(range(2, bits)) + [1]
    barrier = pltpu.get_barrier_semaphore()
    greeted = [above, below] + partners
    greeted.append(quad + 3 - (me - quad))
    for device in greeted:
        pl.semaphore_signal(barrier, inc=1, device_id={"space": device}, device_id_type=MESH)
    pl.semaphore_wait(barrier, len(greeted))

    def remote(source, target, send_sem, recv_sem, device):
        return pltpu.make_async_remote_copy(
            src_ref=source,
            dst_ref=target,
            send_sem=send_sem,
            recv_sem=recv_sem,
            device_id={"space": device},
            device_id_type=MESH,
        )

    pending = []

    def halo_copies(step):
        source = (planes, first_field, final_field)[step]
        if step == 2:
            return [
                remote(
                    source.at[0], final_field.at[2], halo_send.at[4], halo_recv.at[4], below
                )
            ]
        return [
            remote(
                source.at[edge],
                halo.at[step, edge],
                halo_send.at[2 * step + edge],
                halo_recv.at[2 * step + edge],
                (below, above)[edge],
            )
            for edge in range(2)
        ]

    def spread_links(t, device):
        return remote(
            links_ref.at[t],
            plane_links.at[side],
            spread_link_send.at[t],
            spread_link_recv.at[side],
            device,
        )

    def spread_field(t, device):
        return remote(
            eig_ref.at[t], planes.at[side], spread_send.at[t], spread_recv.at[side], device
        )

    targets = [quad + 2 * t + own_t for t in range(slices)]
    for t in range(slices):

        @pl.when(targets[t] != me)
        def _(t=t):
            spread_links(t, targets[t]).start()
            spread_field(t, targets[t]).start()

        @pl.when(targets[t] == me)
        def _(t=t):
            pltpu.make_async_copy(
                links_ref.at[t], plane_links.at[side], spread_link_recv.at[side]
            ).start()
            pltpu.make_async_copy(
                eig_ref.at[t], planes.at[side], spread_recv.at[side]
            ).start()

    for slot in range(2):
        pltpu.make_async_copy(
            links_ref.at[0], plane_links.at[slot], spread_link_recv.at[slot]
        ).wait()
    link_copy = remote(plane_links.at[1, 2], z_below, link_send, link_recv, above)
    link_copy.start()
    pending.append(link_copy)

    row = lax.broadcasted_iota(jnp.int32, (SITES, SITES), 0)
    col = lax.broadcasted_iota(jnp.int32, (SITES, SITES), 1)

    def next_x(site):
        return (site + LY) % SITES

    def next_y(site):
        return (site // LY) * LY + (site + 1) % LY

    ahead_x = col == next_x(row)
    ahead_y = col == next_y(row)
    behind_x = row == next_x(col)
    behind_y = row == next_y(col)
    same = row == col

    def build_planes(t, carry):
        columns[...] = jnp.zeros(columns.shape, F32)
        columns[0:18, :] = plane_links[t, 0]
        columns[24:42, :] = plane_links[t, 1]
        turned = columns[...].T
        for c in range(3):
            for d in range(3):
                blocks = []
                for part, sign in ((0, 1.0), (1, -1.0)):
                    here = part * 9 + c * 3 + d
                    there = part * 9 + d * 3 + c
                    block = jnp.where(ahead_x, turned[:, here : here + 1], 0.0)
                    block = jnp.where(ahead_y, turned[:, 24 + here : 25 + here], block)
                    block = jnp.where(behind_x, sign * plane_links[t, 0, there : there + 1, :], block)
                    block = jnp.where(behind_y, sign * plane_links[t, 1, there : there + 1, :], block)
                    blocks.append(block)
                put_complex(plane_ops, (t,), c, d, *blocks)
                blocks = [
                    jnp.where(same, plane_links[t, 2, p * 9 + c * 3 + d : p * 9 + c * 3 + d + 1, :], 0.0)
                    for p in range(2)
                ]
                put_complex(up_ops, (t,), c, d, *blocks)
        return carry

    def build_hops(index, carry):
        t = index // 2
        k = index % 2
        direction = directions_ref[k]
        target = jnp.where(direction == 0, next_x(col), jnp.where(direction == 1, next_y(col), col))
        reached = row == target
        own = plane_links.at[t]
        values = own[direction]
        for c in range(3):
            for d in range(3):
                there = d * 3 + c
                put_complex(
                    hop_ops,
                    (t, k),
                    c,
                    d,
                    jnp.where(reached, values[there : there + 1, :], 0.0),
                    jnp.where(reached, -values[9 + there : 10 + there, :], 0.0),
                )
        return carry

    def build_down(slot, values_of):
        for c in range(3):
            for d in range(3):
                there = d * 3 + c
                put_complex(
                    down_ops,
                    (slot,),
                    c,
                    d,
                    jnp.where(same, values_of(there), 0.0),
                    jnp.where(same, -values_of(9 + there), 0.0),
                )

    lax.fori_loop(0, slices, build_planes, 0)
    lax.fori_loop(0, 2 * slices, build_hops, 0)
    link_copy.wait_recv()
    build_down(0, lambda j: z_below[j : j + 1, :])
    build_down(1, lambda j: plane_links[0, 2, j : j + 1, :])
    for slot in range(2):
        pltpu.make_async_copy(
            eig_ref.at[0], planes.at[slot], spread_recv.at[slot]
        ).wait()
    for copy in halo_copies(0):
        copy.start()
        pending.append(copy)

    def dot(left_side, right_side):
        return jnp.dot(left_side, right_side, preferred_element_type=F32)

    for step in range(2):
        current = (planes, first_field)[step]
        following = (first_field, final_field)[step]
        copies = halo_copies(step)
        later = halo_copies(step + 1)

        def plane_part(slot, carry, current=current):
            accum[slot] = dot(plane_ops[slot], current[slot])
            return carry

        lax.fori_loop(0, 2, plane_part, 0)
        accum[0] += dot(up_ops[0], current[1])
        accum[1] += dot(down_ops[1], current[0])
        for slot in range(2):
            copies[1 - slot].wait_recv()
            edge_ops = (down_ops, up_ops)[slot]
            total = accum[slot] + dot(edge_ops[slot], halo[step, 1 - slot])
            center = current[slot].astype(F32)
            following[slot] = (center + smear_weight * (total - 6.0 * center)).astype(BF16)
            if slot < len(later):
                later[slot].start()
                pending.append(later[slot])

    def hop_part(index, carry):
        t = index // 2
        k = index % 2
        shifted[t, k] = dot(hop_ops[t, k], final_field[t]).astype(BF16)
        return carry

    lax.fori_loop(0, 2 * slices, hop_part, 0)

    def inner(left_side, right_side):
        return lax.dot_general(
            left_side, right_side, (((0,), (0,)), ((), ())), preferred_element_type=F32
        )

    halo_copies(2)[0].wait_recv()

    def sums(k, carry):
        ahead = jnp.where(directions_ref[k] == 2, 1, 0)
        half = ROWS // 2
        real_part = 0.0
        imag_part = 0.0
        for slot in range(2):
            field = final_field[slot + ahead]
            hopped = shifted[slot, k]
            real_part += inner(hopped, field)
            imag_part += inner(hopped[:half], field[half:]) - inner(hopped[half:], field[:half])
        real_part = real_part - real_part.T
        imag_part = imag_part + imag_part.T
        for block in range(count):
            place = place_of(block, order)
            rows = slice(block * owned, (block + 1) * owned)
            partial_sums[place, 2 * k] = real_part[rows]
            partial_sums[place, 2 * k + 1] = imag_part[rows]
        return carry

    lax.fori_loop(0, 2, sums, 0)

    base = 0
    size = count
    for bit in order[:-1]:
        size //= 2
        kept = base + my_bits[bit] * size
        given = base + (1 - my_bits[bit]) * size
        offset = count - 2 * size
        window = pl.ds(offset, size)
        send_buf[window] = partial_sums[pl.ds(given, size)].astype(BF16)
        copy = remote(
            send_buf.at[window],
            recv_buf.at[window],
            sum_send.at[bit],
            sum_recv.at[bit],
            partners[bit],
        )
        copy.start()
        pending.append(copy)
        copy.wait_recv()
        partial_sums[pl.ds(kept, size)] += recv_buf[window].astype(F32)
        base = kept

    mine = pl.ds(4 * own_t, 4)
    own_rows = partial_sums[pl.ds(base, 2)] * scale
    gathered[pl.ds(base, 2), mine] = own_rows.astype(BF16)
    owned_ref[mine] = partial_sums[base + own_t] * scale
    size = 2
    for bit in list(reversed(order[1:-1])) + [1, 0]:
        window = pl.ds((base // size) * size, size)
        block = gathered.at[window] if bit == 0 else gathered.at[window, mine]
        copy = remote(block, block, gather_send.at[bit], gather_recv.at[bit], partners[bit])
        copy.start()
        pending.append(copy)
        copy.wait_recv()
        if bit == 1:
            other = pl.ds(4 - 4 * own_t, 4)
            owned_ref[other] = gathered[base + own_t, other].astype(F32)
        else:
            size *= 2
    for block in range(count):
        place = place_of(block, order)
        panels_ref[:, block * owned : (block + 1) * owned, :] = gathered[place]
    for copy in pending:
        copy.wait_send()
    for t in range(slices):

        @pl.when(targets[t] != me)
        def _(t=t):
            spread_links(t, targets[t]).wait_send()
            spread_field(t, targets[t]).wait_send()


def pair_kernel(scale, pairs_ref, panels_ref, peram_ref, out_ref):
    p = pl.program_id(0)
    sink = pairs_ref[p, 1]
    source = pairs_ref[p, 0]

    def dot(left_side, right_side):
        return jnp.dot(left_side, right_side, preferred_element_type=F32)

    def dot_adjoint(left_side, right_side):
        return lax.dot_general(
            left_side, right_side, (((1,), (1,)), ((), ())), preferred_element_type=F32
        )

    left_real = panels_ref[sink * 4]
    left_imag = panels_ref[sink * 4 + 1]
    right_real = panels_ref[source * 4 + 2]
    right_imag = panels_ref[source * 4 + 3]
    peram_real = peram_ref[0, 0]
    peram_imag = peram_ref[0, 1]
    first_real = (dot(left_real, peram_real) - dot(left_imag, peram_imag)).astype(BF16)
    first_imag = (dot(left_real, peram_imag) + dot(left_imag, peram_real)).astype(BF16)
    second_real = dot(first_real, right_real) - dot(first_imag, right_imag)
    second_imag = dot(first_real, right_imag) + dot(first_imag, right_real)
    second_real = (second_real * scale).astype(BF16)
    second_imag = (second_imag * scale).astype(BF16)
    out_ref[0, 0] = (
        dot_adjoint(second_real, peram_real) + dot_adjoint(second_imag, peram_imag)
    ).astype(BF16)
    out_ref[0, 1] = (
        dot_adjoint(second_imag, peram_real) - dot_adjoint(second_real, peram_imag)
    ).astype(BF16)


def body(eigvecs, links, directions, pairs, perambulators):
    slices = eigvecs.shape[0]
    planes = eigvecs.shape[3]
    nvec = eigvecs.shape[5]
    count = lax.axis_size("space")
    bits = count.bit_length() - 1
    owned = nvec // count
    assert planes == 1 and slices == 2 and 2**bits == count and bits > 2
    eig = eigvecs.reshape(slices, ROWS, nvec)
    link_rows = links.astype(F32).reshape(slices, 3, 18, SITES)
    site_scale = (6.0 * planes * count * LX * LY) ** (-0.5)
    vmem = pl.BlockSpec(memory_space=pltpu.VMEM)
    smem = pl.BlockSpec(memory_space=pltpu.SMEM)
    dma = pltpu.SemaphoreType.DMA
    field = (slices, ROWS, nvec)
    square = (ROWS, ROWS)
    owned_rows, panels = pl.pallas_call(
        functools.partial(field_kernel, count, site_scale),
        out_shape=(
            jax.ShapeDtypeStruct((4 * slices, owned, nvec), F32),
            jax.ShapeDtypeStruct((4 * slices, nvec, nvec), BF16),
        ),
        in_specs=[smem, vmem, vmem],
        out_specs=(vmem, vmem),
        scratch_shapes=[
            pltpu.VMEM((18, SITES), F32),
            pltpu.VMEM((SITES, SITES), F32),
            pltpu.VMEM((slices, *square), BF16),
            pltpu.VMEM((slices, *square), BF16),
            pltpu.VMEM((slices, *square), BF16),
            pltpu.VMEM((slices, 2, *square), BF16),
            pltpu.VMEM((2, *field), BF16),
            pltpu.VMEM(field, BF16),
            pltpu.VMEM((3, ROWS, nvec), BF16),
            pltpu.VMEM(field, F32),
            pltpu.VMEM((slices, 2, ROWS, nvec), BF16),
            pltpu.VMEM((count, 4, owned, nvec), F32),
            pltpu.VMEM((count, 4, owned, nvec), BF16),
            pltpu.VMEM((count, 4, owned, nvec), BF16),
            pltpu.VMEM((count, 4 * slices, owned, nvec), BF16),
            pltpu.VMEM(field, BF16),
            pltpu.VMEM((2, 3, 18, SITES), F32),
            dma((2,)),
            dma((2,)),
            dma((2,)),
            dma((2,)),
            dma,
            dma,
            dma((5,)),
            dma((5,)),
            dma((bits,)),
            dma((bits,)),
            dma((bits,)),
            dma((bits,)),
        ],
        compiler_params=pltpu.CompilerParams(
            collective_id=0, has_side_effects=True, vmem_limit_bytes=60000 * 1024
        ),
        name="fields",
    )(directions, eig, link_rows)

    pair_scale = (2.0 * nvec) ** (-0.5)
    local_pairs = perambulators.shape[0]
    pair_matrices = pl.pallas_call(
        functools.partial(pair_kernel, pair_scale),
        out_shape=jax.ShapeDtypeStruct(perambulators.shape, BF16),
        grid=(local_pairs,),
        in_specs=[
            smem,
            pl.BlockSpec((4 * slices, nvec, nvec), lambda p: (0, 0, 0)),
            pl.BlockSpec((1, 2, nvec, nvec), lambda p: (p, 0, 0, 0)),
        ],
        out_specs=pl.BlockSpec((1, 2, nvec, nvec), lambda p: (p, 0, 0, 0)),
        name="pairs",
    )(pairs, panels, perambulators)
    return owned_rows.reshape(slices, 2, 2, owned, nvec), pair_matrices


def solution(mesh):
    placed = (
        P("groups", None, None, "space", None, None),
        P("groups", None, None, None, None, "space", None),
        P("groups"),
        P(("groups", "space"), None),
        P(("groups", "space"), None, None, None),
    )
    return jax.shard_map(
        body,
        mesh=mesh,
        in_specs=placed,
        out_specs=(
            P("groups", None, None, "space", None),
            P(("groups", "space"), None, None, None),
        ),
        check_vma=False,
    )
```

```python
import functools

import jax
import jax.numpy as jnp
from jax import lax
from jax.experimental import pallas as pl
from jax.experimental.pallas import tpu as pltpu
from jax.sharding import PartitionSpec as P

LX = 16
LY = 8
SITES = LX * LY
ROWS = 6 * SITES

smear_weight = 0.12
MESH = pl.DeviceIdType.MESH
F32 = jnp.float32
BF16 = jnp.bfloat16


def place_of(value, order):
    result = 0
    for bit in order:
        result = result * 2 + (value >> bit) % 2
    return result


def put_complex(ref, lead, out_color, in_color, real_block, imag_block):
    top = slice(out_color * SITES, (out_color + 1) * SITES)
    low = slice((3 + out_color) * SITES, (4 + out_color) * SITES)
    left = slice(in_color * SITES, (in_color + 1) * SITES)
    right = slice((3 + in_color) * SITES, (4 + in_color) * SITES)
    real_block = real_block.astype(BF16)
    ref[(*lead, top, left)] = real_block
    ref[(*lead, low, right)] = real_block
    ref[(*lead, top, right)] = (-imag_block).astype(BF16)
    ref[(*lead, low, left)] = imag_block.astype(BF16)


def field_kernel(
    count,
    scale,
    directions_ref,
    eig_ref,
    links_ref,
    owned_ref,
    panels_ref,
    z_below,
    columns,
    plane_ops,
    up_ops,
    down_ops,
    hop_ops,
    halo,
    first_field,
    final_field,
    accum,
    shifted,
    partial_sums,
    send_buf,
    recv_buf,
    gathered,
    planes,
    plane_links,
    spread_send,
    spread_recv,
    spread_link_send,
    spread_link_recv,
    link_send,
    link_recv,
    halo_send,
    halo_recv,
    sum_send,
    sum_recv,
    gather_send,
    gather_recv,
):
    slices = eig_ref.shape[0]
    nvec = eig_ref.shape[2]
    bits = count.bit_length() - 1
    owned = nvec // count
    me = lax.axis_index("space")
    my_bits = [(me // 2**bit) % 2 for bit in range(bits)]
    partners = [me + 2**bit * (1 - 2 * my_bits[bit]) for bit in range(bits)]
    side, own_t = my_bits[0], my_bits[1]
    quad = (me // 4) * 4
    above = (me + 1 + 2 * side) % count
    below = (me + count - 3 + 2 * side) % count
    order = [0] + list(range(2, bits)) + [1]
    barrier = pltpu.get_barrier_semaphore()
    greeted = [above, below] + partners
    greeted.append(quad + 3 - (me - quad))
    for device in greeted:
        pl.semaphore_signal(barrier, inc=1, device_id={"space": device}, device_id_type=MESH)
    pl.semaphore_wait(barrier, len(greeted))

    def remote(source, target, send_sem, recv_sem, device):
        return pltpu.make_async_remote_copy(
            src_ref=source,
            dst_ref=target,
            send_sem=send_sem,
            recv_sem=recv_sem,
            device_id={"space": device},
            device_id_type=MESH,
        )

    pending = []

    def halo_copies(step):
        source = (planes, first_field, final_field)[step]
        if step == 2:
            return [
                remote(
                    source.at[0], final_field.at[2], halo_send.at[4], halo_recv.at[4], below
                )
            ]
        return [
            remote(
                source.at[edge],
                halo.at[step, edge],
                halo_send.at[2 * step + edge],
                halo_recv.at[2 * step + edge],
                (below, above)[edge],
            )
            for edge in range(2)
        ]

    def spread_links(t, device):
        return remote(
            links_ref.at[t],
            plane_links.at[side],
            spread_link_send.at[t],
            spread_link_recv.at[side],
            device,
        )

    def spread_field(t, device):
        return remote(
            eig_ref.at[t], planes.at[side], spread_send.at[t], spread_recv.at[side], device
        )

    targets = [quad + 2 * t + own_t for t in range(slices)]
    for t in range(slices):

        @pl.when(targets[t] != me)
        def _(t=t):
            spread_links(t, targets[t]).start()
            spread_field(t, targets[t]).start()

        @pl.when(targets[t] == me)
        def _(t=t):
            pltpu.make_async_copy(
                links_ref.at[t], plane_links.at[side], spread_link_recv.at[side]
            ).start()
            pltpu.make_async_copy(
                eig_ref.at[t], planes.at[side], spread_recv.at[side]
            ).start()

    for slot in range(2):
        pltpu.make_async_copy(
            links_ref.at[0], plane_links.at[slot], spread_link_recv.at[slot]
        ).wait()
    link_copy = remote(plane_links.at[1, 2], z_below, link_send, link_recv, above)
    link_copy.start()
    pending.append(link_copy)

    row = lax.broadcasted_iota(jnp.int32, (SITES, SITES), 0)
    col = lax.broadcasted_iota(jnp.int32, (SITES, SITES), 1)

    def next_x(site):
        return (site + LY) % SITES

    def next_y(site):
        return (site // LY) * LY + (site + 1) % LY

    ahead_x = col == next_x(row)
    ahead_y = col == next_y(row)
    behind_x = row == next_x(col)
    behind_y = row == next_y(col)
    same = row == col

    def build_planes(t, carry):
        columns[...] = jnp.zeros(columns.shape, F32)
        columns[0:18, :] = plane_links[t, 0]
        columns[24:42, :] = plane_links[t, 1]
        turned = columns[...].T
        for c in range(3):
            for d in range(3):
                blocks = []
                for part, sign in ((0, 1.0), (1, -1.0)):
                    here = part * 9 + c * 3 + d
                    there = part * 9 + d * 3 + c
                    block = jnp.where(ahead_x, turned[:, here : here + 1], 0.0)
                    block = jnp.where(ahead_y, turned[:, 24 + here : 25 + here], block)
                    block = jnp.where(behind_x, sign * plane_links[t, 0, there : there + 1, :], block)
                    block = jnp.where(behind_y, sign * plane_links[t, 1, there : there + 1, :], block)
                    blocks.append(block)
                put_complex(plane_ops, (t,), c, d, *blocks)
                blocks = [
                    jnp.where(same, plane_links[t, 2, p * 9 + c * 3 + d : p * 9 + c * 3 + d + 1, :], 0.0)
                    for p in range(2)
                ]
                put_complex(up_ops, (t,), c, d, *blocks)
        return carry

    def build_hops(index, carry):
        t = index // 2
        k = index % 2
        direction = directions_ref[k]
        target = jnp.where(direction == 0, next_x(col), jnp.where(direction == 1, next_y(col), col))
        reached = row == target
        own = plane_links.at[t]
        values = own[direction]
        for c in range(3):
            for d in range(3):
                there = d * 3 + c
                put_complex(
                    hop_ops,
                    (t, k),
                    c,
                    d,
                    jnp.where(reached, values[there : there + 1, :], 0.0),
                    jnp.where(reached, -values[9 + there : 10 + there, :], 0.0),
                )
        return carry

    def build_down(slot, values_of):
        for c in range(3):
            for d in range(3):
                there = d * 3 + c
                put_complex(
                    down_ops,
                    (slot,),
                    c,
                    d,
                    jnp.where(same, values_of(there), 0.0),
                    jnp.where(same, -values_of(9 + there), 0.0),
                )

    lax.fori_loop(0, slices, build_planes, 0)
    lax.fori_loop(0, 2 * slices, build_hops, 0)
    link_copy.wait_recv()
    build_down(0, lambda j: z_below[j : j + 1, :])
    build_down(1, lambda j: plane_links[0, 2, j : j + 1, :])
    for slot in range(2):
        pltpu.make_async_copy(
            eig_ref.at[0], planes.at[slot], spread_recv.at[slot]
        ).wait()
    for copy in halo_copies(0):
        copy.start()
        pending.append(copy)

    def dot(left_side, right_side):
        return jnp.dot(left_side, right_side, preferred_element_type=F32)

    for step in range(2):
        current = (planes, first_field)[step]
        following = (first_field, final_field)[step]
        copies = halo_copies(step)
        later = halo_copies(step + 1)

        def plane_part(slot, carry, current=current):
            accum[slot] = dot(plane_ops[slot], current[slot])
            return carry

        lax.fori_loop(0, 2, plane_part, 0)
        accum[0] += dot(up_ops[0], current[1])
        accum[1] += dot(down_ops[1], current[0])
        for slot in range(2):
            copies[1 - slot].wait_recv()
            edge_ops = (down_ops, up_ops)[slot]
            total = accum[slot] + dot(edge_ops[slot], halo[step, 1 - slot])
            center = current[slot].astype(F32)
            following[slot] = (center + smear_weight * (total - 6.0 * center)).astype(BF16)
            if slot < len(later):
                later[slot].start()
                pending.append(later[slot])

    def hop_part(index, carry):
        t = index // 2
        k = index % 2
        shifted[t, k] = dot(hop_ops[t, k], final_field[t]).astype(BF16)
        return carry

    lax.fori_loop(0, 2 * slices, hop_part, 0)

    def inner(left_side, right_side):
        return lax.dot_general(
            left_side, right_side, (((0,), (0,)), ((), ())), preferred_element_type=F32
        )

    halo_copies(2)[0].wait_recv()

    def sums(k):
        ahead = jnp.where(directions_ref[k] == 2, 1, 0)
        half = ROWS // 2
        real_part = 0.0
        imag_part = 0.0
        for slot in range(2):
            field = final_field[slot + ahead]
            hopped = shifted[slot, k]
            real_part += inner(hopped, field)
            imag_part += inner(hopped[:half], field[half:]) - inner(hopped[half:], field[:half])
        real_part = real_part - real_part.T
        imag_part = imag_part + imag_part.T
        for block in range(count):
            place = place_of(block, order)
            rows = slice(block * owned, (block + 1) * owned)
            partial_sums[k, place, 0] = real_part[rows]
            partial_sums[k, place, 1] = imag_part[rows]

    bases = [0]
    sizes = [count]
    for bit in order[:-1]:
        sizes.append(sizes[-1] // 2)
        bases.append(bases[-1] + my_bits[bit] * sizes[-1])

    def sum_copy(k, level):
        bit = order[level]
        size = sizes[level + 1]
        window = pl.ds(count - 2 * size, size)
        return window, remote(
            send_buf.at[k, window],
            recv_buf.at[k, window],
            sum_send.at[k, level],
            sum_recv.at[k, level],
            partners[bit],
        )

    def send_sum(k, level):
        size = sizes[level + 1]
        given = bases[level] + (1 - my_bits[order[level]]) * size
        window, copy = sum_copy(k, level)
        send_buf[k, window] = partial_sums[k, pl.ds(given, size)].astype(BF16)
        copy.start()
        pending.append(copy)

    def take_sum(k, level):
        window, copy = sum_copy(k, level)
        copy.wait_recv()
        kept = pl.ds(bases[level + 1], sizes[level + 1])
        partial_sums[k, kept] += recv_buf[k, window].astype(F32)

    base = bases[-1]
    levels = len(order) - 1
    gather_order = list(reversed(order[1:-1])) + [1, 0]
    gather_sizes = [2 ** (1 + step) for step in range(levels)] + [count // 2]

    def gather_copy(k, step):
        bit = gather_order[step]
        size = gather_sizes[step]
        window = pl.ds((base // size) * size, size)
        block = gathered.at[k, window] if bit == 0 else gathered.at[k, window, own_t]
        return remote(
            block, block, gather_send.at[k, step], gather_recv.at[k, step], partners[bit]
        )

    def send_gather(k, step):
        copy = gather_copy(k, step)
        copy.start()
        pending.append(copy)

    for k in range(2):
        sums(k)
        send_sum(k, 0)
    for level in range(levels):
        for k in range(2):
            take_sum(k, level)
            if level + 1 < levels:
                send_sum(k, level + 1)
            else:
                gathered[k, pl.ds(base, 2), own_t] = (
                    partial_sums[k, pl.ds(base, 2)] * scale
                ).astype(BF16)
                send_gather(k, 0)
                owned_ref[own_t, k] = partial_sums[k, base + own_t] * scale
    for step, bit in enumerate(gather_order):
        for k in range(2):
            gather_copy(k, step).wait_recv()
            if step + 1 < len(gather_order):
                send_gather(k, step + 1)
            if bit == 1:
                owned_ref[1 - own_t, k] = gathered[k, base + own_t, 1 - own_t].astype(F32)
    for block in range(count):
        place = place_of(block, order)
        for k in range(2):
            panels_ref[:, k, :, block * owned : (block + 1) * owned, :] = gathered[k, place]
    for copy in pending:
        copy.wait_send()
    for t in range(slices):

        @pl.when(targets[t] != me)
        def _(t=t):
            spread_links(t, targets[t]).wait_send()
            spread_field(t, targets[t]).wait_send()


def pair_kernel(scale, pairs_ref, panels_ref, peram_ref, out_ref):
    p = pl.program_id(0)
    sink = pairs_ref[p, 1]
    source = pairs_ref[p, 0]

    def dot(left_side, right_side):
        return jnp.dot(left_side, right_side, preferred_element_type=F32)

    def dot_adjoint(left_side, right_side):
        return lax.dot_general(
            left_side, right_side, (((1,), (1,)), ((), ())), preferred_element_type=F32
        )

    left_real = panels_ref[sink, 0, 0]
    left_imag = panels_ref[sink, 0, 1]
    right_real = panels_ref[source, 1, 0]
    right_imag = panels_ref[source, 1, 1]
    peram_real = peram_ref[0, 0]
    peram_imag = peram_ref[0, 1]
    first_real = (dot(left_real, peram_real) - dot(left_imag, peram_imag)).astype(BF16)
    first_imag = (dot(left_real, peram_imag) + dot(left_imag, peram_real)).astype(BF16)
    second_real = dot(first_real, right_real) - dot(first_imag, right_imag)
    second_imag = dot(first_real, right_imag) + dot(first_imag, right_real)
    second_real = (second_real * scale).astype(BF16)
    second_imag = (second_imag * scale).astype(BF16)
    out_ref[0, 0] = (
        dot_adjoint(second_real, peram_real) + dot_adjoint(second_imag, peram_imag)
    ).astype(BF16)
    out_ref[0, 1] = (
        dot_adjoint(second_imag, peram_real) - dot_adjoint(second_real, peram_imag)
    ).astype(BF16)


def body(eigvecs, links, directions, pairs, perambulators):
    slices = eigvecs.shape[0]
    planes = eigvecs.shape[3]
    nvec = eigvecs.shape[5]
    count = lax.axis_size("space")
    bits = count.bit_length() - 1
    owned = nvec // count
    assert planes == 1 and slices == 2 and 2**bits == count and bits > 2
    eig = eigvecs.reshape(slices, ROWS, nvec)
    link_rows = links.astype(F32).reshape(slices, 3, 18, SITES)
    site_scale = (6.0 * planes * count * LX * LY) ** (-0.5)
    vmem = pl.BlockSpec(memory_space=pltpu.VMEM)
    smem = pl.BlockSpec(memory_space=pltpu.SMEM)
    dma = pltpu.SemaphoreType.DMA
    field = (slices, ROWS, nvec)
    square = (ROWS, ROWS)
    owned_rows, panels = pl.pallas_call(
        functools.partial(field_kernel, count, site_scale),
        out_shape=(
            jax.ShapeDtypeStruct((slices, 2, 2, owned, nvec), F32),
            jax.ShapeDtypeStruct((slices, 2, 2, nvec, nvec), BF16),
        ),
        in_specs=[smem, vmem, vmem],
        out_specs=(vmem, vmem),
        scratch_shapes=[
            pltpu.VMEM((18, SITES), F32),
            pltpu.VMEM((SITES, SITES), F32),
            pltpu.VMEM((slices, *square), BF16),
            pltpu.VMEM((slices, *square), BF16),
            pltpu.VMEM((slices, *square), BF16),
            pltpu.VMEM((slices, 2, *square), BF16),
            pltpu.VMEM((2, *field), BF16),
            pltpu.VMEM(field, BF16),
            pltpu.VMEM((3, ROWS, nvec), BF16),
            pltpu.VMEM(field, F32),
            pltpu.VMEM((slices, 2, ROWS, nvec), BF16),
            pltpu.VMEM((2, count, 2, owned, nvec), F32),
            pltpu.VMEM((2, count, 2, owned, nvec), BF16),
            pltpu.VMEM((2, count, 2, owned, nvec), BF16),
            pltpu.VMEM((2, count, slices, 2, owned, nvec), BF16),
            pltpu.VMEM(field, BF16),
            pltpu.VMEM((2, 3, 18, SITES), F32),
            dma((2,)),
            dma((2,)),
            dma((2,)),
            dma((2,)),
            dma,
            dma,
            dma((5,)),
            dma((5,)),
            dma((2, bits)),
            dma((2, bits)),
            dma((2, bits)),
            dma((2, bits)),
        ],
        compiler_params=pltpu.CompilerParams(
            collective_id=0, has_side_effects=True, vmem_limit_bytes=60000 * 1024
        ),
        name="fields",
    )(directions, eig, link_rows)

    pair_scale = (2.0 * nvec) ** (-0.5)
    local_pairs = perambulators.shape[0]
    pair_matrices = pl.pallas_call(
        functools.partial(pair_kernel, pair_scale),
        out_shape=jax.ShapeDtypeStruct(perambulators.shape, BF16),
        grid=(local_pairs,),
        in_specs=[
            smem,
            pl.BlockSpec((slices, 2, 2, nvec, nvec), lambda p: (0, 0, 0, 0, 0)),
            pl.BlockSpec((1, 2, nvec, nvec), lambda p: (p, 0, 0, 0)),
        ],
        out_specs=pl.BlockSpec((1, 2, nvec, nvec), lambda p: (p, 0, 0, 0)),
        name="pairs",
    )(pairs, panels, perambulators)
    return owned_rows, pair_matrices


def solution(mesh):
    placed = (
        P("groups", None, None, "space", None, None),
        P("groups", None, None, None, None, "space", None),
        P("groups"),
        P(("groups", "space"), None),
        P(("groups", "space"), None, None, None),
    )
    return jax.shard_map(
        body,
        mesh=mesh,
        in_specs=placed,
        out_specs=(
            P("groups", None, None, "space", None),
            P(("groups", "space"), None, None, None),
        ),
        check_vma=False,
    )
```
